32 devices in a mesh: dp: 8 (over z, core), tensor: 4 (over y, x).
Axes of the slice: x: 2, y: 2, z: 4, core: 2. Of those that a mesh axis runs over, the one named last changes fastest.
Arguments:
- hidden_acts: bfloat16 [16384, 14336], P('dp', 'tensor'), may hold values from -6 to 6
- out_grads: bfloat16 [16384, 4096], P('dp', 'tensor'), may hold values from -6 to 6
- proj_in: bfloat16 [14336, 64], P('tensor'), may hold values from -0.046875 to 0.046875
- proj_out: bfloat16 [4096, 64], P('tensor'), may hold values from -0.09375 to 0.09375
- segments: int32 [32, 16384], P(None, 'dp'), may hold values from 0 to 1, as said below
- doc_counts: int32 [8], P('dp'), may hold values from 10 to 32
Outputs:
- doc_grads: bfloat16 [256, 4096], P('dp', 'tensor')
- fisher: float32 [4096, 4096], P('dp', 'tensor')
The draws below stay inside these ranges and needn't reach their ends.
Inputs may be any that keep to these rules, and one draw needn't show every extreme that they name: `segments`: every token belongs to exactly one slot of its shard; within one shard's 2048 tokens the slots 0 to 31 are contiguous runs in that order, each holding at least one token.
All inputs are finite; a program needn't handle non-finite values.
Results may differ from the reference program's by a relative error of at most 0.0062.
Values may be sent and summed in bfloat16 or wider, within the bound.
No kernel may reach another device: no remote copies, remote signals or barrier semaphores. Data moves between devices by JAX's collectives and lax.ppermute only.
A program may use at most 64 MiB of HBM per device.

```python
import jax
import jax.numpy as jnp
from jax import lax

D = 4096
FF = 14336
RANK = 64
TOK_DEV = 2048
DOCS_DEV = 32
TOKENS = 16384


def doc_layout(key):
    shards = TOKENS // TOK_DEV

    def one_shard(subkey):
        shuffled = jax.random.permutation(subkey, TOK_DEV - 1)
        cut_points = shuffled[:DOCS_DEV - 1] + 1
        boundary = jnp.zeros((TOK_DEV,), jnp.int32).at[cut_points].set(1)
        slot_of = jnp.cumsum(boundary).astype(jnp.int32)
        return (jnp.arange(DOCS_DEV, dtype=jnp.int32)[:, None] == slot_of[None, :]).astype(jnp.int32)
    blocks = jax.vmap(one_shard)(jax.random.split(key, shards))
    return blocks.transpose(1, 0, 2).reshape(DOCS_DEV, TOKENS)


def draw_segments(key, part):
    return doc_layout(jax.random.fold_in(key, 11))


def draw_doc_counts(key, part):
    shards = TOKENS // TOK_DEV
    least_docs = max(1, DOCS_DEV // 3)
    position = jnp.arange(shards, dtype=jnp.int32)
    rising = least_docs + position * (DOCS_DEV - least_docs) // max(shards - 1, 1)
    reach = max(1, DOCS_DEV // 12)
    jitter = jax.random.randint(jax.random.fold_in(key, 23), (shards,), -reach, reach + 1, dtype=jnp.int32)
    counts_drawn = jnp.clip(rising + jitter, least_docs, DOCS_DEV)
    counts_drawn = counts_drawn.at[0].set(least_docs).at[shards - 1].set(DOCS_DEV)
    return counts_drawn.astype(jnp.int32)


def shard_levels(own_key, shape, cuts, smallest, high):
    def one(dim, shards_of):
        draws = jax.random.uniform(jax.random.fold_in(jax.random.fold_in(own_key, 6), dim), (shards_of,), jnp.float32, smallest / len(cuts), high / len(cuts))
        return jnp.repeat(jnp.exp(draws), shape[dim] // shards_of).reshape((-1,) + (1,) * (len(shape) - dim - 1))

    factor_of = one(*cuts[0])
    for cut in cuts[1:]:
        factor_of = factor_of * one(*cut)
    return factor_of


def noise(key, dims, deviation, bound, cuts=(), kind=jnp.bfloat16):
    gain = shard_levels(key, dims, cuts, -0.22, 0.18) if cuts else 1.0
    drawn = jax.random.normal(key, dims, jnp.float32) * deviation * gain
    return jnp.minimum(jnp.maximum(drawn, -bound), bound).astype(kind)


def setup_inputs(seed: int = 0) -> dict:
    arg_keys = jax.random.split(jax.random.key(seed), 7)
    return {
        "hidden_acts": noise(arg_keys[0], (TOKENS, FF), 1.0, 6.0, ((0, 8), (1, 4))),
        "out_grads": noise(arg_keys[1], (TOKENS, D), 1.0, 6.0, ((0, 8), (1, 4))),
        "proj_in": noise(arg_keys[2], (FF, RANK), FF ** -0.5, 0.046875, ((0, 4),)),
        "proj_out": noise(arg_keys[3], (D, RANK), D ** -0.5, 0.09375, ((0, 4),)),
        "segments": draw_segments(jax.random.fold_in(arg_keys[6], 71), 0),
        "doc_counts": draw_doc_counts(jax.random.fold_in(arg_keys[6], 71), 0),
    }


def reference(hidden_acts, out_grads, proj_in, proj_out, segments, doc_counts):
    shard_total = doc_counts.shape[0]
    shard_tokens = hidden_acts.shape[0] // shard_total
    x_proj = jnp.dot(hidden_acts, proj_in, preferred_element_type=jnp.float32)
    dy_proj = jnp.dot(out_grads, proj_out, preferred_element_type=jnp.float32)
    doc_index = jnp.arange(segments.shape[0], dtype=jnp.int32)

    def per_shard(shard_idx):
        offset = (shard_idx * shard_tokens).astype(jnp.int32)
        x_rows = lax.dynamic_slice_in_dim(x_proj, offset, shard_tokens, 0)
        dy_rows = lax.dynamic_slice_in_dim(dy_proj, offset, shard_tokens, 0)
        seg_rows = lax.dynamic_slice_in_dim(segments, offset, shard_tokens, 1)
        live_docs = (doc_index < doc_counts[shard_idx]).astype(jnp.int32)
        seg_live = seg_rows * live_docs[:, None]
        outer = (dy_rows[:, :, None] * x_rows[:, None, :]).reshape(shard_tokens, -1).astype(jnp.bfloat16)
        doc_terms = jnp.dot(seg_live.astype(jnp.bfloat16), outer, preferred_element_type=jnp.float32)
        return doc_terms, jnp.sum(seg_live).astype(jnp.float32)

    doc_sums, live_tokens = lax.map(per_shard, jnp.arange(shard_total, dtype=jnp.int32))
    doc_grads = doc_sums.reshape(-1, doc_sums.shape[-1]).astype(jnp.bfloat16)
    total_tokens = jnp.sum(live_tokens)
    fisher = jnp.dot(doc_grads.T, doc_grads, preferred_element_type=jnp.float32) / total_tokens
    return doc_grads, fisher
```

```python
import functools

import jax
import jax.numpy as jnp
from jax import lax
from jax.experimental import pallas as pl
from jax.experimental.pallas import tpu as pltpu
from jax.sharding import PartitionSpec as P

BF16 = jnp.bfloat16
F32 = jnp.float32
NT = (((1,), (1,)), ((), ()))
TN = (((0,), (0,)), ((), ()))


def peer_of(idx, step, size):
    if size & (size - 1) == 0:
        return idx ^ step
    return lax.rem(step + size - idx, size)


def swap(value, axis, step):
    size = lax.axis_size(axis)
    pairs = []
    for idx in range(size):
        other = idx ^ step if size & (size - 1) == 0 else (step - idx) % size
        pairs.append((idx, other))
    return lax.ppermute(value, axis, pairs)


def smem():
    return pl.BlockSpec(memory_space=pltpu.SMEM)


def dy_kernel(tensor_size, pos_ref, counts_ref, seg_ref, grads_ref, proj_ref, *rest):
    outs, count_ref, weights = rest[:tensor_size], rest[tensor_size], rest[tensor_size + 1]
    step = pl.program_id(0)
    rank = proj_ref.shape[0]
    part = rank // tensor_size

    @pl.when(step == 0)
    def _():
        row = lax.broadcasted_iota(jnp.int32, (rank, rank), 0)
        col = lax.broadcasted_iota(jnp.int32, (rank, rank), 1)
        source = peer_of(pos_ref[0], row // part, tensor_size) * part + row % part
        pick = jnp.where(col == source, 1.0, 0.0).astype(BF16)
        weights[...] = jnp.dot(pick, proj_ref[...], preferred_element_type=F32).astype(BF16)
        count_ref[...] = jnp.zeros_like(count_ref)

    partial = lax.dot_general(weights[...], grads_ref[...], NT, preferred_element_type=F32)
    for k in range(tensor_size):
        outs[k][...] = partial[k * part : (k + 1) * part, :].astype(outs[k].dtype)
    docs = lax.broadcasted_iota(jnp.int32, seg_ref.shape, 0)
    live = jnp.where(docs < counts_ref[0], seg_ref[...], 0)
    count_ref[...] += jnp.sum(live).astype(F32)


def dy_partials(pos, counts, seg, grads, proj_t, tensor_size):
    tokens, width = grads.shape
    rank = proj_t.shape[0]
    part = rank // tensor_size
    tile = min(512, tokens)
    docs = seg.shape[0]
    outs = [
        jax.ShapeDtypeStruct((part, tokens), F32 if k == 0 else BF16) for k in range(tensor_size)
    ]
    return pl.pallas_call(
        functools.partial(dy_kernel, tensor_size),
        grid=(tokens // tile,),
        in_specs=[
            smem(),
            smem(),
            pl.BlockSpec((docs, tile), lambda i: (0, i)),
            pl.BlockSpec((tile, width), lambda i: (i, 0)),
            pl.BlockSpec((rank, width), lambda i: (0, 0)),
        ],
        out_specs=[pl.BlockSpec((part, tile), lambda i: (0, i)) for _ in outs]
        + [pl.BlockSpec((8, 128), lambda i: (0, 0))],
        out_shape=outs + [jax.ShapeDtypeStruct((8, 128), F32)],
        scratch_shapes=[pltpu.VMEM((rank, width), BF16)],
        cost_estimate=pl.CostEstimate(
            flops=2 * tokens * width * rank, bytes_accessed=2 * tokens * width, transcendentals=0
        ),
        name="dy_partials",
    )(pos, counts, seg, grads, proj_t)


def x_kernel(steps, pos_ref, acts_ref, proj_ref, *outs):
    step, sub = pl.program_id(0), pl.program_id(1)
    tile = acts_ref.shape[0]
    partial = lax.dot_general(proj_ref[...], acts_ref[...], NT, preferred_element_type=F32)
    cols = pl.ds(pl.multiple_of(sub * tile, tile), tile)
    for n in range(len(steps)):

        @pl.when(step == n)
        def _():
            outs[n][:, cols] = partial.astype(outs[n].dtype)


def x_partials(pos, acts, proj_t, steps, tensor_size, dtype):
    tokens, width = acts.shape
    rank = proj_t.shape[0]
    chunk = tokens // tensor_size
    tile = min(256, chunk)
    per_chunk = chunk // tile
    first = steps[0]

    def token_block(n, j, pos_ref):
        return peer_of(pos_ref[0], n + first, tensor_size) * per_chunk + j, 0

    outs = [jax.ShapeDtypeStruct((rank, chunk), dtype) for _ in steps]
    flops = 2 * chunk * len(steps) * width * rank
    return pl.pallas_call(
        functools.partial(x_kernel, steps),
        grid_spec=pltpu.PrefetchScalarGridSpec(
            num_scalar_prefetch=1,
            grid=(len(steps), per_chunk),
            in_specs=[
                pl.BlockSpec((tile, width), token_block),
                pl.BlockSpec((rank, width), lambda n, j, p: (0, 0)),
            ],
            out_specs=[pl.BlockSpec((rank, chunk), lambda n, j, p: (0, 0)) for _ in outs],
        ),
        out_shape=outs,
        cost_estimate=pl.CostEstimate(
            flops=flops, bytes_accessed=2 * chunk * len(steps) * width, transcendentals=0
        ),
        name="x_partials",
    )(pos, acts, proj_t)


def docs_kernel(tensor_size, pos_ref, counts_ref, seg_ref, *rest):
    dy_parts, xs = rest[:tensor_size], rest[tensor_size : 2 * tensor_size]
    out_ref, dy_ref, sums_ref = rest[2 * tensor_size :]
    docs, tokens = seg_ref.shape
    part = dy_parts[0].shape[0]
    rows = dy_ref.shape[0]
    rank, chunk = xs[0].shape
    total = dy_parts[0][...]
    for other in dy_parts[1:]:
        total = total + other[...].astype(F32)
    if rows > part:
        total = jnp.concatenate([total, jnp.zeros((rows - part, tokens), F32)], axis=0)
    dy_ref[...] = total
    sums = jnp.zeros((docs * rows, rank), F32)
    doc = lax.broadcasted_iota(jnp.int32, (docs, chunk), 0)
    for k in range(tensor_size):
        start = peer_of(pos_ref[0], k, tensor_size) * chunk
        cols = pl.ds(pl.multiple_of(start, chunk), chunk)
        seg = jnp.where(doc < counts_ref[0], seg_ref[:, cols], 0).astype(F32).astype(BF16)
        dy = dy_ref[:, cols]
        high = dy.astype(BF16)
        low = (dy - high.astype(F32)).astype(BF16)
        for piece in (high, low):
            masked = (seg[:, None, :] * piece[None, :, :]).reshape(docs * rows, chunk)
            sums = sums + lax.dot_general(masked, xs[k][...], NT, preferred_element_type=F32)
    sums_ref[...] = sums
    lanes = 128 // rank
    for a in range(0, part, lanes):
        pieces = [sums_ref[pl.ds(a + n, docs, stride=rows), :] for n in range(lanes)]
        wide = pieces[0] if lanes == 1 else jnp.concatenate(pieces, axis=1)
        out_ref[:, a * rank : (a + lanes) * rank] = wide.astype(BF16)


def doc_sums(pos, counts, seg, dy_parts, xs):
    tensor_size = len(xs)
    docs, tokens = seg.shape
    part = dy_parts[0].shape[0]
    rank = xs[0].shape[0]
    rows = -(-part // 16) * 16
    vmem = pl.BlockSpec(memory_space=pltpu.VMEM)
    return pl.pallas_call(
        functools.partial(docs_kernel, tensor_size),
        in_specs=[smem(), smem()] + [vmem] * (1 + 2 * tensor_size),
        out_specs=vmem,
        out_shape=jax.ShapeDtypeStruct((docs, part * rank), BF16),
        scratch_shapes=[pltpu.VMEM((rows, tokens), F32), pltpu.VMEM((docs * rows, rank), F32)],
        cost_estimate=pl.CostEstimate(
            flops=4 * docs * rows * tokens * rank, bytes_accessed=1 << 20, transcendentals=0
        ),
        name="doc_sums",
    )(pos, counts, seg, *dy_parts, *xs)


def fisher_kernel(shards, total_ref, *rest):
    rows, cols, out_ref = rest[:shards], rest[shards : 2 * shards], rest[2 * shards]
    left = jnp.concatenate([r[...] for r in rows], axis=0)
    right = jnp.concatenate([c[...] for c in cols], axis=0)
    product = lax.dot_general(left, right, TN, preferred_element_type=F32)
    out_ref[...] = product / total_ref[0:1, 0:1]


def fisher_block(total, rows, cols):
    shards = len(rows)
    docs, height = rows[0].shape
    width = cols[0].shape[1]
    tile = min(128, height)
    return pl.pallas_call(
        functools.partial(fisher_kernel, shards),
        grid=(height // tile,),
        in_specs=[pl.BlockSpec((8, 128), lambda i: (0, 0))]
        + [pl.BlockSpec((docs, tile), lambda i: (0, i)) for _ in rows]
        + [pl.BlockSpec((docs, width), lambda i: (0, 0)) for _ in cols],
        out_specs=pl.BlockSpec((tile, width), lambda i: (i, 0)),
        out_shape=jax.ShapeDtypeStruct((height, width), F32),
        cost_estimate=pl.CostEstimate(
            flops=2 * docs * shards * height * width,
            bytes_accessed=4 * height * width,
            transcendentals=0,
        ),
        name="fisher_block",
    )(total, *rows, *cols)


def per_device(hidden_acts, out_grads, proj_in, proj_out, segments, doc_counts):
    tensor_size, dp_size = lax.axis_size("tensor"), lax.axis_size("dp")
    pos = lax.axis_index("tensor").astype(jnp.int32).reshape(1)
    shard = lax.axis_index("dp").astype(jnp.int32)
    steps = range(1, tensor_size)

    *dy_parts, count = dy_partials(
        pos, doc_counts, segments, out_grads, proj_out.T, tensor_size
    )
    dy_parts = [dy_parts[0]] + [swap(dy_parts[k], "tensor", k) for k in steps]

    step = 1
    while step < dp_size:
        count = count + swap(count, "dp", step)
        step *= 2

    proj_t = proj_in.T
    sent = x_partials(pos, hidden_acts, proj_t, tuple(steps), tensor_size, BF16)
    received = [swap(sent[k - 1], "tensor", k) for k in steps]
    (own,) = x_partials(pos, hidden_acts, proj_t, (0,), tensor_size, F32)
    for other in received:
        own = own + other.astype(F32)
    own = own.astype(BF16)
    xs = [own] + [swap(own, "tensor", k) for k in steps]

    grads = doc_sums(pos, doc_counts, segments, dy_parts, xs)
    cols = [grads]
    for j in range(2, dp_size, 2):
        cols += [None, swap(grads, "dp", j)]
    cols.append(None)
    for j in range(1, dp_size, 2):
        cols[j] = swap(cols[j - 1], "dp", 1)
    blocks = jnp.stack([grads] + [swap(grads, "tensor", k) for k in steps])
    share = dp_size // tensor_size
    height = grads.shape[1] // share
    rows = []
    for j in range(dp_size):
        target = peer_of(shard, j, dp_size)
        block = peer_of(pos[0], target // share, tensor_size)
        piece = lax.dynamic_slice(
            blocks, (block, 0, target % share * height), (1, grads.shape[0], height)
        )[0]
        rows.append(piece if j == 0 else swap(piece, "dp", j))
    return grads, fisher_block(count, rows, cols)


def solution(mesh):
    return jax.shard_map(
        per_device,
        mesh=mesh,
        in_specs=(
            P("dp", "tensor"),
            P("dp", "tensor"),
            P("tensor", None),
            P("tensor", None),
            P(None, "dp"),
            P("dp"),
        ),
        out_specs=(P("dp", "tensor"), P("dp", "tensor")),
        check_vma=False,
    )
```

```python
import functools

import jax
import jax.numpy as jnp
from jax import lax
from jax.experimental import pallas as pl
from jax.experimental.pallas import tpu as pltpu
from jax.sharding import PartitionSpec as P

BF16 = jnp.bfloat16
F32 = jnp.float32
NT = (((1,), (1,)), ((), ()))
TN = (((0,), (0,)), ((), ()))
SMEM = pl.BlockSpec(memory_space=pltpu.SMEM)
VMEM = pl.BlockSpec(memory_space=pltpu.VMEM)
DIGITS = (65536, 256, 1)
DIGIT_ROWS = 8


def swap(value, axis, step):
    return lax.ppermute(value, axis, [(i, i ^ step) for i in range(lax.axis_size(axis))])


def peers_kernel(pos_ref, acts_ref, grads_ref, proj_in_ref, proj_out_ref, *rest):
    outs, own_ref, weights = rest[:-2], rest[-2], rest[-1]
    size = len(outs) + 1
    step = pl.program_id(0)
    rank = proj_out_ref.shape[0]
    part = rank // size

    @pl.when(step == 0)
    def _():
        row = lax.broadcasted_iota(jnp.int32, (rank, rank), 0)
        col = lax.broadcasted_iota(jnp.int32, (rank, rank), 1)
        source = (pos_ref[0] ^ (row // part)) * part + row % part
        pick = jnp.where(col == source, 1.0, 0.0).astype(BF16)
        weights[...] = jnp.dot(pick, proj_out_ref[...], preferred_element_type=F32).astype(BF16)

    dy = lax.dot_general(weights[...], grads_ref[...], NT, preferred_element_type=F32)
    for n in range(size):

        @pl.when(step == n)
        def _():
            lines = slice(n * part, (n + 1) * part)
            own_ref[lines, :] = dy[:part, :]
            for k in range(1, size):
                lines = slice(rank + n * part, rank + (n + 1) * part)
                outs[k - 1][lines, :] = dy[k * part : (k + 1) * part, :].astype(BF16)
            if n + 1 < size:
                x = lax.dot_general(
                    proj_in_ref[...], acts_ref[...], NT, preferred_element_type=F32
                )
                outs[n][:rank, :] = x.astype(BF16)


def peer_messages(pos, acts, grads, proj_in_t, proj_out_t, size):
    tokens, acts_width = acts.shape
    grads_width = grads.shape[1]
    rank = proj_in_t.shape[0]
    chunk = tokens // size
    whole = lambda n, p: (0, 0)
    outs = [jax.ShapeDtypeStruct((2 * rank, chunk), BF16)] * (size - 1)
    outs += [jax.ShapeDtypeStruct((rank, chunk), F32)]
    return pl.pallas_call(
        peers_kernel,
        grid_spec=pltpu.PrefetchScalarGridSpec(
            num_scalar_prefetch=1,
            grid=(size,),
            in_specs=[
                pl.BlockSpec(
                    (chunk, acts_width), lambda n, p: (p[0] ^ jnp.minimum(n + 1, size - 1), 0)
                ),
                pl.BlockSpec((chunk, grads_width), lambda n, p: (n, 0)),
                pl.BlockSpec((rank, acts_width), whole),
                pl.BlockSpec((rank, grads_width), whole),
            ],
            out_specs=[pl.BlockSpec(o.shape, whole) for o in outs],
            scratch_shapes=[pltpu.VMEM((rank, grads_width), BF16)],
        ),
        out_shape=outs,
        cost_estimate=pl.CostEstimate(
            flops=2 * tokens * rank * (acts_width + grads_width),
            bytes_accessed=2 * tokens * (acts_width + grads_width),
            transcendentals=0,
        ),
        name="peer_messages",
    )(pos, acts, grads, proj_in_t, proj_out_t)


def own_kernel(pos_ref, acts_ref, proj_ref, out_ref):
    out_ref[...] = lax.dot_general(proj_ref[...], acts_ref[...], NT, preferred_element_type=F32)


def own_partial(pos, acts, proj_t, size):
    tokens, width = acts.shape
    rank = proj_t.shape[0]
    chunk = tokens // size
    tile = min(256, chunk)
    tiles = chunk // tile
    return pl.pallas_call(
        own_kernel,
        grid_spec=pltpu.PrefetchScalarGridSpec(
            num_scalar_prefetch=1,
            grid=(tiles,),
            in_specs=[
                pl.BlockSpec((tile, width), lambda n, p: (p[0] * tiles + n, 0)),
                pl.BlockSpec((rank, width), lambda n, p: (0, 0)),
            ],
            out_specs=pl.BlockSpec((rank, tile), lambda n, p: (0, n)),
        ),
        out_shape=jax.ShapeDtypeStruct((rank, chunk), F32),
        cost_estimate=pl.CostEstimate(
            flops=2 * chunk * width * rank, bytes_accessed=2 * chunk * width, transcendentals=0
        ),
        name="own_partial",
    )(pos, acts, proj_t)


def docs_kernel(size, pos_ref, counts_ref, seg_ref, dy_own_ref, *rest):
    messages, xs = rest[: size - 1], rest[size - 1 : 2 * size - 1]
    grads_ref, shared_ref, dy_ref, sums_ref = rest[2 * size - 1 :]
    docs, tokens = seg_ref.shape
    rank, chunk = xs[0].shape
    part = rank // size
    rows = dy_ref.shape[0] // size
    total = dy_own_ref[...]
    for message in messages:
        total = total + message[rank:, :].astype(F32)
    for n in range(size):
        lines = total[n * part : (n + 1) * part, :]
        if rows > part:
            lines = jnp.concatenate([lines, jnp.zeros((rows - part, chunk), F32)], axis=0)
        dy_ref[n * rows : (n + 1) * rows, :] = lines
    sums = jnp.zeros((docs * rows, rank), F32)
    doc = lax.broadcasted_iota(jnp.int32, (docs, chunk), 0)
    live_tokens = jnp.zeros((docs, chunk), jnp.int32)
    for k in range(size):
        block = pos_ref[0] ^ k
        cols = pl.ds(pl.multiple_of(block * chunk, chunk), chunk)
        seg = jnp.where(doc < counts_ref[0], seg_ref[:, cols], 0)
        live_tokens = live_tokens + seg
        seg = seg.astype(F32).astype(BF16)
        dy = dy_ref[pl.ds(pl.multiple_of(block * rows, rows), rows), :]
        high = dy.astype(BF16)
        low = (dy - high.astype(F32)).astype(BF16)
        for piece in (high, low):
            masked = (seg[:, None, :] * piece[None, :, :]).reshape(docs * rows, chunk)
            sums = sums + lax.dot_general(masked, xs[k][...], NT, preferred_element_type=F32)
    sums_ref[...] = sums
    lanes = 128 // rank
    for a in range(0, part, lanes):
        pieces = [sums_ref[pl.ds(a + n, docs, stride=rows), :] for n in range(lanes)]
        wide = pieces[0] if lanes == 1 else jnp.concatenate(pieces, axis=1)
        wide = wide.astype(BF16)
        grads_ref[:, a * rank : (a + lanes) * rank] = wide
        shared_ref[:docs, a * rank : (a + lanes) * rank] = wide
    left = jnp.sum(live_tokens)
    row = lax.broadcasted_iota(jnp.int32, (DIGIT_ROWS, part * rank), 0)
    digits = jnp.zeros(row.shape, jnp.int32)
    for n, unit in enumerate(DIGITS):
        digit = left // unit
        left = left - digit * unit
        digits = jnp.where(row == n, digit, digits)
    shared_ref[docs:, :] = digits.astype(F32).astype(BF16)


def doc_sums(pos, counts, seg, dy_own, messages, xs):
    size = len(xs)
    docs, tokens = seg.shape
    rank, chunk = xs[0].shape
    part = rank // size
    rows = -(-part // 16) * 16
    return pl.pallas_call(
        functools.partial(docs_kernel, size),
        in_specs=[SMEM, SMEM] + [VMEM] * (1 + 2 * size),
        out_specs=[VMEM, VMEM],
        out_shape=[
            jax.ShapeDtypeStruct((docs, part * rank), BF16),
            jax.ShapeDtypeStruct((docs + DIGIT_ROWS, part * rank), BF16),
        ],
        scratch_shapes=[
            pltpu.VMEM((rows * size, chunk), F32),
            pltpu.VMEM((docs * rows, rank), F32),
        ],
        cost_estimate=pl.CostEstimate(
            flops=4 * docs * rows * tokens * rank, bytes_accessed=1 << 20, transcendentals=0
        ),
        name="doc_sums",
    )(pos, counts, seg, dy_own, *messages, *xs)


def fisher_kernel(shards, half_ref, *rest):
    rows, cols, out_ref = rest[:shards], rest[shards : 2 * shards], rest[2 * shards]
    docs = rows[0].shape[0]
    left = jnp.concatenate([r[...] for r in rows], axis=0)
    right = jnp.concatenate([c[:docs, :] for c in cols], axis=0)
    product = lax.dot_general(left, right, TN, preferred_element_type=F32)
    total = jnp.zeros((1, 1), F32)
    for c in cols:
        digits = c[docs:, 0:1].astype(F32)
        for n, unit in enumerate(DIGITS):
            total = total + digits[n : n + 1, :] * float(unit)
    out_ref[...] = product / total


def fisher_block(half, rows, cols):
    shards = len(rows)
    docs, width = rows[0].shape
    height = width // 2
    tile = min(128, height)
    tiles = height // tile
    return pl.pallas_call(
        functools.partial(fisher_kernel, shards),
        grid_spec=pltpu.PrefetchScalarGridSpec(
            num_scalar_prefetch=1,
            grid=(tiles,),
            in_specs=[pl.BlockSpec((docs, tile), lambda i, h: (0, h[0] * tiles + i))] * shards
            + [pl.BlockSpec((docs + DIGIT_ROWS, width), lambda i, h: (0, 0))] * shards,
            out_specs=pl.BlockSpec((tile, width), lambda i, h: (i, 0)),
        ),
        out_shape=jax.ShapeDtypeStruct((height, width), F32),
        cost_estimate=pl.CostEstimate(
            flops=2 * docs * shards * height * width,
            bytes_accessed=4 * height * width,
            transcendentals=0,
        ),
        name="fisher_block",
    )(half, *rows, *cols)


def per_device(hidden_acts, out_grads, proj_in, proj_out, segments, doc_counts):
    size, dp_size = lax.axis_size("tensor"), lax.axis_size("dp")
    assert dp_size == 2 * size
    pos = lax.axis_index("tensor").astype(jnp.int32)
    shard = lax.axis_index("dp").astype(jnp.int32)
    pair, half = shard // 2, shard % 2
    steps = range(1, size)
    pos1, half1 = pos.reshape(1), half.reshape(1)

    proj_in_t = proj_in.T
    *messages, dy_own = peer_messages(pos1, hidden_acts, out_grads, proj_in_t, proj_out.T, size)
    messages = [swap(messages[k - 1], "tensor", k) for k in steps]
    x = own_partial(pos1, hidden_acts, proj_in_t, size)
    rank = x.shape[0]
    for message in messages:
        x = x + message[:rank].astype(F32)
    x = x.astype(BF16)
    xs = [x] + [swap(x, "tensor", k) for k in steps]
    grads, shared = doc_sums(pos1, doc_counts, segments, dy_own, messages, xs)

    cols = {0: shared}
    for j in steps:
        low = j & -j
        cols[j] = swap(cols[j - low] if j != low else shared, "dp", 2 * low)
    blocks = [grads] + [swap(grads, "tensor", k) for k in steps]
    rows = []
    for j in range(size):
        where = pos ^ pair ^ j
        picked = blocks[0]
        for k in steps:
            picked = jnp.where(where == k, blocks[k], picked)
        rows.append(picked if j == 0 else swap(picked, "dp", 2 * j))
    cols = [cols[j] for j in range(size)]
    cols += [swap(c, "dp", 1) for c in cols]
    rows += [swap(r, "dp", 1) for r in rows]
    return grads, fisher_block(half1, rows, cols)


def solution(mesh):
    return jax.shard_map(
        per_device,
        mesh=mesh,
        in_specs=(
            P("dp", "tensor"),
            P("dp", "tensor"),
            P("tensor", None),
            P("tensor", None),
            P(None, "dp"),
            P("dp"),
        ),
        out_specs=(P("dp", "tensor"), P("dp", "tensor")),
        check_vma=False,
    )
```

```python
import functools

import jax
import jax.numpy as jnp
from jax import lax
from jax.experimental import pallas as pl
from jax.experimental.pallas import tpu as pltpu
from jax.sharding import PartitionSpec as P


BF16 = jnp.bfloat16
F32 = jnp.float32
NT = (((1,), (1,)), ((), ()))
TN = (((0,), (0,)), ((), ()))
SMEM = pl.BlockSpec(memory_space=pltpu.SMEM)
VMEM = pl.BlockSpec(memory_space=pltpu.VMEM)
DIGITS = (65536, 256, 1)
DIGIT_ROWS = 8


def swap(value, axis, step):
    return lax.ppermute(value, axis, [(i, i ^ step) for i in range(lax.axis_size(axis))])


def peers_kernel(pos_ref, acts_ref, grads_ref, proj_in_ref, proj_out_ref, *rest):
    outs, own_ref, weights = rest[:-2], rest[-2], rest[-1]
    size = len(outs) + 1
    step = pl.program_id(0)
    rank = proj_out_ref.shape[0]
    part = rank // size

    @pl.when(step == 0)
    def _():
        row = lax.broadcasted_iota(jnp.int32, (rank, rank), 0)
        col = lax.broadcasted_iota(jnp.int32, (rank, rank), 1)
        source = (pos_ref[0] ^ (row // part)) * part + row % part
        pick = jnp.where(col == source, 1.0, 0.0).astype(BF16)
        weights[...] = jnp.dot(pick, proj_out_ref[...], preferred_element_type=F32).astype(BF16)

    dy = lax.dot_general(weights[...], grads_ref[...], NT, preferred_element_type=F32)
    for n in range(size):

        @pl.when(step == n)
        def _():
            lines = slice(n * part, (n + 1) * part)
            own_ref[lines, :] = dy[:part, :]
            for k in range(1, size):
                lines = slice(rank + n * part, rank + (n + 1) * part)
                outs[k - 1][lines, :] = dy[k * part : (k + 1) * part, :].astype(BF16)
            if n + 1 < size:
                x = lax.dot_general(
                    proj_in_ref[...], acts_ref[...], NT, preferred_element_type=F32
                )
                outs[n][:rank, :] = x.astype(BF16)


def peer_messages(pos, acts, grads, proj_in_t, proj_out_t, size):
    tokens, acts_width = acts.shape
    grads_width = grads.shape[1]
    rank = proj_in_t.shape[0]
    chunk = tokens // size
    whole = lambda n, p: (0, 0)
    outs = [jax.ShapeDtypeStruct((2 * rank, chunk), BF16)] * (size - 1)
    outs += [jax.ShapeDtypeStruct((rank, chunk), F32)]
    return pl.pallas_call(
        peers_kernel,
        grid_spec=pltpu.PrefetchScalarGridSpec(
            num_scalar_prefetch=1,
            grid=(size,),
            in_specs=[
                pl.BlockSpec(
                    (chunk, acts_width), lambda n, p: (p[0] ^ jnp.minimum(n + 1, size - 1), 0)
                ),
                pl.BlockSpec((chunk, grads_width), lambda n, p: (n, 0)),
                pl.BlockSpec((rank, acts_width), whole),
                pl.BlockSpec((rank, grads_width), whole),
            ],
            out_specs=[pl.BlockSpec(o.shape, whole) for o in outs],
            scratch_shapes=[pltpu.VMEM((rank, grads_width), BF16)],
        ),
        out_shape=outs,
        cost_estimate=pl.CostEstimate(
            flops=2 * tokens * rank * (acts_width + grads_width),
            bytes_accessed=2 * tokens * (acts_width + grads_width),
            transcendentals=0,
        ),
        compiler_params=pltpu.CompilerParams(vmem_limit_bytes=58 << 20),
        name="peer_messages",
    )(pos, acts, grads, proj_in_t, proj_out_t)


def own_kernel(pos_ref, acts_ref, proj_ref, out_ref):
    out_ref[...] = lax.dot_general(proj_ref[...], acts_ref[...], NT, preferred_element_type=F32)


def own_partial(pos, acts, proj_t, size):
    tokens, width = acts.shape
    rank = proj_t.shape[0]
    chunk = tokens // size
    tile = min(256, chunk)
    tiles = chunk // tile
    return pl.pallas_call(
        own_kernel,
        grid_spec=pltpu.PrefetchScalarGridSpec(
            num_scalar_prefetch=1,
            grid=(tiles,),
            in_specs=[
                pl.BlockSpec((tile, width), lambda n, p: (p[0] * tiles + n, 0)),
                pl.BlockSpec((rank, width), lambda n, p: (0, 0)),
            ],
            out_specs=pl.BlockSpec((rank, tile), lambda n, p: (0, n)),
        ),
        out_shape=jax.ShapeDtypeStruct((rank, chunk), F32),
        cost_estimate=pl.CostEstimate(
            flops=2 * chunk * width * rank, bytes_accessed=2 * chunk * width, transcendentals=0
        ),
        compiler_params=pltpu.CompilerParams(vmem_limit_bytes=48 << 20),
        name="own_partial",
    )(pos, acts, proj_t)


def docs_kernel(size, pos_ref, counts_ref, seg_ref, dy_own_ref, *rest):
    messages, xs = rest[: size - 1], rest[size - 1 : 2 * size - 1]
    grads_ref, inner_ref, shared_ref, dy_ref, sums_ref = rest[2 * size - 1 :]
    docs, _ = seg_ref.shape
    rank, chunk = xs[0].shape
    part = rank // size
    rows = dy_ref.shape[0] // size
    total = dy_own_ref[...]
    for message in messages:
        total = total + message[rank:, :].astype(F32)
    for n in range(size):
        lines = total[n * part : (n + 1) * part, :]
        if rows > part:
            lines = jnp.concatenate([lines, jnp.zeros((rows - part, chunk), F32)], axis=0)
        dy_ref[n * rows : (n + 1) * rows, :] = lines
    sums = jnp.zeros((docs * rows, rank), F32)
    doc = lax.broadcasted_iota(jnp.int32, (docs, chunk), 0)
    live_tokens = jnp.zeros((docs, chunk), jnp.int32)
    for k in range(size):
        block = pos_ref[0] ^ k
        cols = pl.ds(pl.multiple_of(block * chunk, chunk), chunk)
        seg = jnp.where(doc < counts_ref[0], seg_ref[:, cols], 0)
        live_tokens = live_tokens + seg
        seg = seg.astype(F32).astype(BF16)
        dy = dy_ref[pl.ds(pl.multiple_of(block * rows, rows), rows), :]
        high = dy.astype(BF16)
        low = (dy - high.astype(F32)).astype(BF16)
        for piece in (high, low):
            masked = (seg[:, None, :] * piece[None, :, :]).reshape(docs * rows, chunk)
            sums = sums + lax.dot_general(masked, xs[k][...], NT, preferred_element_type=F32)
    sums_ref[...] = sums
    lanes = 128 // rank
    for a in range(0, part, lanes):
        pieces = [sums_ref[pl.ds(a + n, docs, stride=rows), :] for n in range(lanes)]
        wide = pieces[0] if lanes == 1 else jnp.concatenate(pieces, axis=1)
        wide = wide.astype(BF16)
        span = slice(a * rank, (a + lanes) * rank)
        grads_ref[:, span] = wide
        inner_ref[:, span] = wide
        shared_ref[:docs, span] = wide
    left = jnp.sum(live_tokens)
    row = lax.broadcasted_iota(jnp.int32, (DIGIT_ROWS, part * rank), 0)
    digits = jnp.zeros(row.shape, jnp.int32)
    for n, unit in enumerate(DIGITS):
        digit = left // unit
        left = left - digit * unit
        digits = jnp.where(row == n, digit, digits)
    shared_ref[docs:, :] = digits.astype(F32).astype(BF16)


def doc_sums(pos, counts, seg, dy_own, messages, xs):
    size = len(xs)
    docs, tokens = seg.shape
    rank, chunk = xs[0].shape
    part = rank // size
    rows = -(-part // 16) * 16
    return pl.pallas_call(
        functools.partial(docs_kernel, size),
        in_specs=[SMEM, SMEM] + [VMEM] * (1 + 2 * size),
        out_specs=[VMEM, VMEM, VMEM],
        out_shape=[
            jax.ShapeDtypeStruct((docs, part * rank), BF16),
            jax.ShapeDtypeStruct((docs, part * rank), BF16),
            jax.ShapeDtypeStruct((docs + DIGIT_ROWS, part * rank), BF16),
        ],
        scratch_shapes=[
            pltpu.VMEM((rows * size, chunk), F32),
            pltpu.VMEM((docs * rows, rank), F32),
        ],
        cost_estimate=pl.CostEstimate(
            flops=4 * docs * rows * tokens * rank, bytes_accessed=1 << 20, transcendentals=0
        ),
        compiler_params=pltpu.CompilerParams(vmem_limit_bytes=16 << 20),
        name="doc_sums",
    )(pos, counts, seg, dy_own, *messages, *xs)


def fisher_kernel(shards, half_ref, *rest):
    rows, cols, out_ref = rest[:shards], rest[shards : 2 * shards], rest[2 * shards]
    docs = rows[0].shape[0]
    left = jnp.concatenate([r[...] for r in rows], axis=0)
    right = jnp.concatenate([c[:docs, :] for c in cols], axis=0)
    product = lax.dot_general(left, right, TN, preferred_element_type=F32)
    total = jnp.zeros((1, 1), F32)
    for c in cols:
        digits = c[docs:, 0:1].astype(F32)
        for n, unit in enumerate(DIGITS):
            total = total + digits[n : n + 1, :] * float(unit)
    out_ref[...] = product * (1.0 / total)


def fisher_block(half, rows, cols):
    shards = len(rows)
    docs, width = rows[0].shape
    height = width // 2
    tile = min(256, height)
    tiles = height // tile
    return pl.pallas_call(
        functools.partial(fisher_kernel, shards),
        grid_spec=pltpu.PrefetchScalarGridSpec(
            num_scalar_prefetch=1,
            grid=(tiles,),
            in_specs=[pl.BlockSpec((docs, tile), lambda i, h: (0, h[0] * tiles + i))] * shards
            + [pl.BlockSpec((docs + DIGIT_ROWS, width), lambda i, h: (0, 0))] * shards,
            out_specs=pl.BlockSpec((tile, width), lambda i, h: (i, 0)),
        ),
        out_shape=jax.ShapeDtypeStruct((height, width), F32),
        cost_estimate=pl.CostEstimate(
            flops=2 * docs * shards * height * width,
            bytes_accessed=4 * height * width,
            transcendentals=0,
        ),
        compiler_params=pltpu.CompilerParams(vmem_limit_bytes=16 << 20),
        name="fisher_block",
    )(half, *rows, *cols)


def per_device(hidden_acts, out_grads, proj_in, proj_out, segments, doc_counts):
    size, dp_size = lax.axis_size("tensor"), lax.axis_size("dp")
    assert dp_size == 2 * size
    pos = lax.axis_index("tensor").astype(jnp.int32)
    shard = lax.axis_index("dp").astype(jnp.int32)
    pair, half = shard // 2, shard % 2
    steps = range(1, size)
    pos1, half1 = pos.reshape(1), half.reshape(1)

    proj_in_t = proj_in.T
    *messages, dy_own = peer_messages(pos1, hidden_acts, out_grads, proj_in_t, proj_out.T, size)
    messages = [swap(messages[k - 1], "tensor", k) for k in steps]
    x = own_partial(pos1, hidden_acts, proj_in_t, size)
    rank = x.shape[0]
    for message in messages:
        x = x + message[:rank].astype(F32)
    x = x.astype(BF16)
    xs = [x] + [swap(x, "tensor", k) for k in steps]
    grads, inner, shared = doc_sums(pos1, doc_counts, segments, dy_own, messages, xs)

    cols = {0: shared}
    for j in steps:
        low = j & -j
        cols[j] = swap(cols[j - low] if j != low else shared, "dp", 2 * low)
    blocks = [inner] + [swap(inner, "tensor", k) for k in steps]
    rows = []
    for j in range(size):
        where = pos ^ pair ^ j
        picked = blocks[0]
        for k in steps:
            picked = jnp.where(where == k, blocks[k], picked)
        rows.append(picked if j == 0 else swap(picked, "dp", 2 * j))
    cols = [cols[j] for j in range(size)]
    cols += [swap(c, "dp", 1) for c in cols]
    rows += [swap(r, "dp", 1) for r in rows]
    return grads, fisher_block(half1, rows, cols)


def solution(mesh):
    return jax.shard_map(
        per_device,
        mesh=mesh,
        in_specs=(
            P("dp", "tensor"),
            P("dp", "tensor"),
            P("tensor", None),
            P("tensor", None),
            P(None, "dp"),
            P("dp"),
        ),
        out_specs=(P("dp", "tensor"), P("dp", "tensor")),
        check_vma=False,
    )
```

```python
import functools

import jax
import jax.numpy as jnp
from jax import lax
from jax.experimental import pallas as pl
from jax.experimental.pallas import tpu as pltpu
from jax.sharding import PartitionSpec as P


BF16 = jnp.bfloat16
F32 = jnp.float32
NT = (((1,), (1,)), ((), ()))
TN = (((0,), (0,)), ((), ()))
SMEM = pl.BlockSpec(memory_space=pltpu.SMEM)
VMEM = pl.BlockSpec(memory_space=pltpu.VMEM)
HBM = pl.BlockSpec(memory_space=pltpu.HBM)
DIGITS = (65536, 256, 1)
DIGIT_ROWS = 8
FIRST_GRANT = 58 << 20
SECOND_GRANT = 48 << 20


def swap(value, axis, step):
    return lax.ppermute(value, axis, [(i, i ^ step) for i in range(lax.axis_size(axis))])


def stream(copies, depth, work):
    for copy in copies[:depth]:
        copy.start()
    for n, copy in enumerate(copies):
        copy.wait()
        if n + depth < len(copies):
            copies[n + depth].start()
        work(n)


def project(proj_ref, piece_ref, start, sums_ref, done):
    stop = start + piece_ref.shape[1]
    partial = lax.dot_general(
        proj_ref[:, start:stop], piece_ref[...], NT, preferred_element_type=F32
    )
    if start > 0:
        partial = sums_ref[...] + partial
    if stop < proj_ref.shape[1]:
        sums_ref[...] = partial
    else:
        done(partial)


def chunk_copies(acts_ref, block, chunk, buffers, sems, first):
    width = buffers.shape[2]
    rows = pl.ds(pl.multiple_of(block * chunk, chunk), chunk)
    return [
        pltpu.make_async_copy(
            acts_ref.at[rows, n * width : (n + 1) * width],
            buffers.at[first + n],
            sems.at[first + n],
        )
        for n in range(acts_ref.shape[1] // width)
    ]


def pieces_of(width, most):
    return max(n for n in range(1, most + 1) if width % (128 * n) == 0)


def peers_kernel(size, pos_ref, acts_ref, proj_ref, *rest):
    outs, (buffers, sums_ref, sems) = rest[: size - 1], rest[size - 1 :]
    chunk = buffers.shape[1]
    pieces = buffers.shape[0] // (size - 1)
    copies = []
    for k in range(1, size):
        block = pos_ref[0] ^ k
        copies += chunk_copies(acts_ref, block, chunk, buffers, sems, (k - 1) * pieces)

    def work(n):
        def done(x):
            outs[n // pieces][...] = x.astype(BF16)

        piece = buffers.at[n]
        project(proj_ref, piece, n % pieces * piece.shape[1], sums_ref, done)

    stream(copies, 3, work)


def peer_partials(pos, acts, proj_t, size):
    tokens, width = acts.shape
    rank = proj_t.shape[0]
    chunk = tokens // size
    pieces = pieces_of(width, 2)
    count = (size - 1) * pieces
    outs = [jax.ShapeDtypeStruct((rank, chunk), BF16)] * (size - 1)
    return pl.pallas_call(
        functools.partial(peers_kernel, size),
        in_specs=[SMEM, HBM, VMEM],
        out_specs=[VMEM] * len(outs),
        out_shape=outs,
        scratch_shapes=[
            pltpu.VMEM((count, chunk, width // pieces), BF16),
            pltpu.VMEM((rank, chunk), F32),
            pltpu.SemaphoreType.DMA((count,)),
        ],
        cost_estimate=pl.CostEstimate(
            flops=2 * chunk * (size - 1) * rank * width,
            bytes_accessed=2 * chunk * (size - 1) * width,
            transcendentals=0,
        ),
        compiler_params=pltpu.CompilerParams(vmem_limit_bytes=FIRST_GRANT),
        name="peer_partials",
    )(pos, acts, proj_t)


def own_kernel(size, pos_ref, acts_ref, grads_ref, proj_in_ref, proj_out_ref, *rest):
    own_ref, dy_refs = rest[0], rest[1 : size + 1]
    weights, acts_buf, grads_buf, sums_ref, acts_sem, grads_sem = rest[size + 1 :]
    pos = pos_ref[0]
    rank = proj_out_ref.shape[0]
    part = rank // size
    chunk = acts_buf.shape[1]
    parts, span, _ = grads_buf.shape
    copies = [
        pltpu.make_async_copy(
            grads_ref.at[n * span : (n + 1) * span], grads_buf.at[n], grads_sem.at[n]
        )
        for n in range(parts)
    ]
    copies += chunk_copies(acts_ref, pos, chunk, acts_buf, acts_sem, 0)

    def work(n):
        if n == 0:
            row = lax.broadcasted_iota(jnp.int32, (rank, rank), 0)
            col = lax.broadcasted_iota(jnp.int32, (rank, rank), 1)
            source = (pos ^ (row // part)) * part + row % part
            pick = jnp.where(col == source, 1.0, 0.0).astype(BF16)
            weights[...] = jnp.dot(
                pick, proj_out_ref[...], preferred_element_type=F32
            ).astype(BF16)
        if n < parts:
            dy = lax.dot_general(weights[...], grads_buf[n], NT, preferred_element_type=F32)
            for m in range(span // chunk):
                block = dy[:, m * chunk : (m + 1) * chunk]
                first = (n * (span // chunk) + m) * part
                for k in range(size):
                    lines = block[k * part : (k + 1) * part, :]
                    dy_refs[k][first : first + part, :] = lines.astype(dy_refs[k].dtype)
        else:

            def done(x):
                own_ref[...] = x

            piece = acts_buf.at[n - parts]
            project(proj_in_ref, piece, (n - parts) * piece.shape[1], sums_ref, done)

    stream(copies, 4, work)


def own_partials(pos, acts, grads, proj_in_t, proj_out_t, size):
    tokens, acts_width = acts.shape
    grads_width = grads.shape[1]
    rank = proj_in_t.shape[0]
    chunk = tokens // size
    pieces = pieces_of(acts_width, 2)
    return pl.pallas_call(
        functools.partial(own_kernel, size),
        in_specs=[SMEM, HBM, HBM, VMEM, VMEM],
        out_specs=[VMEM] * (size + 1),
        out_shape=[jax.ShapeDtypeStruct((rank, chunk), F32)] * 2
        + [jax.ShapeDtypeStruct((rank, chunk), BF16)] * (size - 1),
        scratch_shapes=[
            pltpu.VMEM((rank, grads_width), BF16),
            pltpu.VMEM((pieces, chunk, acts_width // pieces), BF16),
            pltpu.VMEM((2, tokens // 2, grads_width), BF16),
            pltpu.VMEM((rank, chunk), F32),
            pltpu.SemaphoreType.DMA((pieces,)),
            pltpu.SemaphoreType.DMA((2,)),
        ],
        cost_estimate=pl.CostEstimate(
            flops=2 * rank * (chunk * acts_width + tokens * grads_width),
            bytes_accessed=2 * (chunk * acts_width + tokens * grads_width),
            transcendentals=0,
        ),
        compiler_params=pltpu.CompilerParams(vmem_limit_bytes=SECOND_GRANT),
        name="own_partials",
    )(pos, acts, grads, proj_in_t, proj_out_t)


def docs_kernel(size, pos_ref, counts_ref, seg_ref, dy_own_ref, x_own_ref, *rest):
    messages = rest[: size - 1]
    grads_ref, inner_ref, shared_ref, dy_ref, sums_ref = rest[size - 1 :]
    docs, _ = seg_ref.shape
    rank, chunk = x_own_ref.shape
    part = rank // size
    rows = dy_ref.shape[0] // size
    total = dy_own_ref[...]
    for message in messages:
        total = total + message[rank:, :].astype(F32)
    for n in range(size):
        lines = total[n * part : (n + 1) * part, :]
        if rows > part:
            lines = jnp.concatenate([lines, jnp.zeros((rows - part, chunk), F32)], axis=0)
        dy_ref[n * rows : (n + 1) * rows, :] = lines
    sums = jnp.zeros((docs * rows, rank), F32)
    doc = lax.broadcasted_iota(jnp.int32, (docs, chunk), 0)
    live_tokens = jnp.zeros((docs, chunk), jnp.int32)
    for k in range(size):
        block = pos_ref[0] ^ k
        cols = pl.ds(pl.multiple_of(block * chunk, chunk), chunk)
        seg = jnp.where(doc < counts_ref[0], seg_ref[:, cols], 0)
        live_tokens = live_tokens + seg
        seg = seg.astype(F32).astype(BF16)
        dy = dy_ref[pl.ds(pl.multiple_of(block * rows, rows), rows), :]
        high = dy.astype(BF16)
        low = (dy - high.astype(F32)).astype(BF16)
        x = x_own_ref[...] if k == 0 else messages[k - 1][:rank, :]
        for piece in (high, low):
            masked = (seg[:, None, :] * piece[None, :, :]).reshape(docs * rows, chunk)
            sums = sums + lax.dot_general(masked, x, NT, preferred_element_type=F32)
    sums_ref[...] = sums
    lanes = 128 // rank
    for a in range(0, part, lanes):
        pieces = [sums_ref[pl.ds(a + n, docs, stride=rows), :] for n in range(lanes)]
        wide = pieces[0] if lanes == 1 else jnp.concatenate(pieces, axis=1)
        wide = wide.astype(BF16)
        span = slice(a * rank, (a + lanes) * rank)
        grads_ref[:, span] = wide
        inner_ref[:, span] = wide
        shared_ref[:docs, span] = wide
    left = jnp.sum(live_tokens)
    row = lax.broadcasted_iota(jnp.int32, (DIGIT_ROWS, part * rank), 0)
    digits = jnp.zeros(row.shape, jnp.int32)
    for n, unit in enumerate(DIGITS):
        digit = left // unit
        left = left - digit * unit
        digits = jnp.where(row == n, digit, digits)
    shared_ref[docs:, :] = digits.astype(F32).astype(BF16)


def doc_sums(pos, counts, seg, dy_own, x_own, messages):
    size = len(messages) + 1
    docs, tokens = seg.shape
    rank, chunk = x_own.shape
    part = rank // size
    rows = -(-part // 16) * 16
    return pl.pallas_call(
        functools.partial(docs_kernel, size),
        in_specs=[SMEM, SMEM] + [VMEM] * (2 + size),
        out_specs=[VMEM, VMEM, VMEM],
        out_shape=[
            jax.ShapeDtypeStruct((docs, part * rank), BF16),
            jax.ShapeDtypeStruct((docs, part * rank), BF16),
            jax.ShapeDtypeStruct((docs + DIGIT_ROWS, part * rank), BF16),
        ],
        scratch_shapes=[
            pltpu.VMEM((rows * size, chunk), F32),
            pltpu.VMEM((docs * rows, rank), F32),
        ],
        cost_estimate=pl.CostEstimate(
            flops=4 * docs * rows * tokens * rank, bytes_accessed=1 << 20, transcendentals=0
        ),
        compiler_params=pltpu.CompilerParams(vmem_limit_bytes=16 << 20),
        name="doc_sums",
    )(pos, counts, seg, dy_own, x_own, *messages)


def fisher_kernel(shards, half_ref, *rest):
    rows, cols, out_ref = rest[:shards], rest[shards : 2 * shards], rest[2 * shards]
    docs = rows[0].shape[0]
    left = jnp.concatenate([r[...] for r in rows], axis=0)
    right = jnp.concatenate([c[:docs, :] for c in cols], axis=0)
    product = lax.dot_general(left, right, TN, preferred_element_type=F32)
    total = jnp.zeros((1, 1), F32)
    for c in cols:
        digits = c[docs:, 0:1].astype(F32)
        for n, unit in enumerate(DIGITS):
            total = total + digits[n : n + 1, :] * float(unit)
    out_ref[...] = product * (1.0 / total)


def fisher_block(half, rows, cols):
    shards = len(rows)
    docs, width = rows[0].shape
    height = width // 2
    tile = min(256, height)
    tiles = height // tile
    return pl.pallas_call(
        functools.partial(fisher_kernel, shards),
        grid_spec=pltpu.PrefetchScalarGridSpec(
            num_scalar_prefetch=1,
            grid=(tiles,),
            in_specs=[pl.BlockSpec((docs, tile), lambda i, h: (0, h[0] * tiles + i))] * shards
            + [pl.BlockSpec((docs + DIGIT_ROWS, width), lambda i, h: (0, 0))] * shards,
            out_specs=pl.BlockSpec((tile, width), lambda i, h: (i, 0)),
        ),
        out_shape=jax.ShapeDtypeStruct((height, width), F32),
        cost_estimate=pl.CostEstimate(
            flops=2 * docs * shards * height * width,
            bytes_accessed=4 * height * width,
            transcendentals=0,
        ),
        compiler_params=pltpu.CompilerParams(vmem_limit_bytes=16 << 20),
        name="fisher_block",
    )(half, *rows, *cols)


def per_device(hidden_acts, out_grads, proj_in, proj_out, segments, doc_counts):
    size, dp_size = lax.axis_size("tensor"), lax.axis_size("dp")
    assert dp_size == 2 * size
    pos = lax.axis_index("tensor").astype(jnp.int32)
    shard = lax.axis_index("dp").astype(jnp.int32)
    pair, half = shard // 2, shard % 2
    steps = range(1, size)
    pos1, half1 = pos.reshape(1), half.reshape(1)

    proj_in_t = proj_in.T
    partials = peer_partials(pos1, hidden_acts, proj_in_t, size)
    partials = [swap(partials[k - 1], "tensor", k) for k in steps]
    x, dy_own, *dys = own_partials(
        pos1, hidden_acts, out_grads, proj_in_t, proj_out.T, size
    )
    for partial in partials:
        x = x + partial.astype(F32)
    x = x.astype(BF16)
    messages = [swap(jnp.concatenate([x, dys[k - 1]]), "tensor", k) for k in steps]
    grads, inner, shared = doc_sums(pos1, doc_counts, segments, dy_own, x, messages)

    cols = {0: shared}
    for j in steps:
        low = j & -j
        cols[j] = swap(cols[j - low] if j != low else shared, "dp", 2 * low)
    blocks = [inner] + [swap(inner, "tensor", k) for k in steps]
    rows = []
    for j in range(size):
        where = pos ^ pair ^ j
        picked = blocks[0]
        for k in steps:
            picked = jnp.where(where == k, blocks[k], picked)
        rows.append(picked if j == 0 else swap(picked, "dp", 2 * j))
    cols = [cols[j] for j in range(size)]
    cols += [swap(c, "dp", 1) for c in cols]
    rows += [swap(r, "dp", 1) for r in rows]
    return grads, fisher_block(half1, rows, cols)


def solution(mesh):
    return jax.shard_map(
        per_device,
        mesh=mesh,
        in_specs=(
            P("dp", "tensor"),
            P("dp", "tensor"),
            P("tensor", None),
            P("tensor", None),
            P(None, "dp"),
            P("dp"),
        ),
        out_specs=(P("dp", "tensor"), P("dp", "tensor")),
        check_vma=False,
    )
```

```python
import functools

import jax
import jax.numpy as jnp
from jax import lax
from jax.experimental import pallas as pl
from jax.experimental.pallas import tpu as pltpu
from jax.sharding import PartitionSpec as P


BF16 = jnp.bfloat16
F32 = jnp.float32
NT = (((1,), (1,)), ((), ()))
TN = (((0,), (0,)), ((), ()))
SMEM = pl.BlockSpec(memory_space=pltpu.SMEM)
VMEM = pl.BlockSpec(memory_space=pltpu.VMEM)
HBM = pl.BlockSpec(memory_space=pltpu.HBM)
DIGITS = (65536, 256, 1)
DIGIT_ROWS = 8
TILE = 128
FIRST_GRANT = 48 << 20
SECOND_GRANT = 48 << 20


def swap(value, axis, step):
    return lax.ppermute(value, axis, [(i, i ^ step) for i in range(lax.axis_size(axis))])


def stream(copies, depth, work):
    for copy in copies[:depth]:
        copy.start()
    for n, copy in enumerate(copies):
        copy.wait()
        if n + depth < len(copies):
            copies[n + depth].start()
        work(n)


def project(proj_ref, piece_ref, start, sums_ref, done):
    stop = start + piece_ref.shape[1]
    partial = lax.dot_general(
        proj_ref[:, start:stop], piece_ref[...], NT, preferred_element_type=F32
    )
    if start > 0:
        partial = sums_ref[...] + partial
    if stop < proj_ref.shape[1]:
        sums_ref[...] = partial
    else:
        done(partial)


def chunk_copies(acts_ref, block, chunk, buffers, sems, first):
    width = buffers.shape[2]
    rows = pl.ds(pl.multiple_of(block * chunk, chunk), chunk)
    return [
        pltpu.make_async_copy(
            acts_ref.at[rows, n * width : (n + 1) * width],
            buffers.at[first + n],
            sems.at[first + n],
        )
        for n in range(acts_ref.shape[1] // width)
    ]


def pieces_of(width, most):
    return max(n for n in range(1, most + 1) if width % (128 * n) == 0)


def peers_kernel(size, pos_ref, acts_ref, proj_ref, *rest):
    outs, (proj_buf, buffers, sums_ref, sems, proj_sem) = rest[: size - 1], rest[size - 1 :]
    chunk = buffers.shape[1]
    load = pltpu.make_async_copy(proj_ref, proj_buf, proj_sem)
    load.start()
    pieces = buffers.shape[0] // (size - 1)
    copies = []
    for k in range(1, size):
        block = pos_ref[0] ^ k
        copies += chunk_copies(acts_ref, block, chunk, buffers, sems, (k - 1) * pieces)

    def work(n):
        if n == 0:
            load.wait()

        def done(x):
            outs[n // pieces][...] = x.astype(BF16)

        piece = buffers.at[n]
        project(proj_buf, piece, n % pieces * piece.shape[1], sums_ref, done)

    stream(copies, 3, work)


def peer_partials(pos, acts, proj_t, size):
    tokens, width = acts.shape
    rank = proj_t.shape[0]
    chunk = tokens // size
    pieces = pieces_of(width, 2)
    count = (size - 1) * pieces
    outs = [jax.ShapeDtypeStruct((rank, chunk), BF16)] * (size - 1)
    return pl.pallas_call(
        functools.partial(peers_kernel, size),
        in_specs=[SMEM, HBM, HBM],
        out_specs=[VMEM] * len(outs),
        out_shape=outs,
        scratch_shapes=[
            pltpu.VMEM((rank, width), BF16),
            pltpu.VMEM((count, chunk, width // pieces), BF16),
            pltpu.VMEM((rank, chunk), F32),
            pltpu.SemaphoreType.DMA((count,)),
            pltpu.SemaphoreType.DMA,
        ],
        cost_estimate=pl.CostEstimate(
            flops=2 * chunk * (size - 1) * rank * width,
            bytes_accessed=2 * chunk * (size - 1) * width,
            transcendentals=0,
        ),
        compiler_params=pltpu.CompilerParams(vmem_limit_bytes=FIRST_GRANT),
        name="peer_partials",
    )(pos, acts, pltpu.with_memory_space_constraint(proj_t, pltpu.HBM))


def own_kernel(size, pos_ref, acts_ref, grads_ref, proj_in_ref, proj_out_ref, *rest):
    own_ref, dy_refs = rest[0], rest[1 : size + 1]
    weights, acts_buf, sums_ref, acts_sem = rest[size + 1 :]
    pos = pos_ref[0]
    rank = proj_out_ref.shape[0]
    part = rank // size
    chunk = acts_buf.shape[1]
    copies = chunk_copies(acts_ref, pos, chunk, acts_buf, acts_sem, 0)
    for copy in copies:
        copy.start()

    row = lax.broadcasted_iota(jnp.int32, (rank, rank), 0)
    col = lax.broadcasted_iota(jnp.int32, (rank, rank), 1)
    source = (pos ^ (row // part)) * part + row % part
    pick = jnp.where(col == source, 1.0, 0.0).astype(BF16)
    weights[...] = jnp.dot(pick, proj_out_ref[...], preferred_element_type=F32).astype(BF16)
    dy = lax.dot_general(weights[...], grads_ref[...], NT, preferred_element_type=F32)
    for m in range(size):
        for k in range(size):
            lines = dy[k * part : (k + 1) * part, m * chunk : (m + 1) * chunk]
            dy_refs[k][m * part : (m + 1) * part, :] = lines.astype(dy_refs[k].dtype)

    def done(x):
        own_ref[...] = x

    for n, copy in enumerate(copies):
        copy.wait()
        piece = acts_buf.at[n]
        project(proj_in_ref, piece, n * piece.shape[1], sums_ref, done)


def own_partials(pos, acts, grads, proj_in_t, proj_out_t, size):
    tokens, acts_width = acts.shape
    grads_width = grads.shape[1]
    rank = proj_in_t.shape[0]
    chunk = tokens // size
    pieces = pieces_of(acts_width, 2)
    return pl.pallas_call(
        functools.partial(own_kernel, size),
        in_specs=[SMEM, HBM, VMEM, VMEM, VMEM],
        out_specs=[VMEM] * (size + 1),
        out_shape=[jax.ShapeDtypeStruct((rank, chunk), F32)] * 2
        + [jax.ShapeDtypeStruct((rank, chunk), BF16)] * (size - 1),
        scratch_shapes=[
            pltpu.VMEM((rank, grads_width), BF16),
            pltpu.VMEM((pieces, chunk, acts_width // pieces), BF16),
            pltpu.VMEM((rank, chunk), F32),
            pltpu.SemaphoreType.DMA((pieces,)),
        ],
        cost_estimate=pl.CostEstimate(
            flops=2 * rank * (chunk * acts_width + tokens * grads_width),
            bytes_accessed=2 * (chunk * acts_width + tokens * grads_width),
            transcendentals=0,
        ),
        compiler_params=pltpu.CompilerParams(vmem_limit_bytes=SECOND_GRANT),
        name="own_partials",
    )(pos, acts, grads, proj_in_t, proj_out_t)


def docs_kernel(size, pos_ref, counts_ref, seg_ref, dy_own_ref, x_own_ref, *rest):
    messages = rest[: size - 1]
    inner_ref, shared_ref, dy_ref, sums_ref = rest[size - 1 :]
    docs, _ = seg_ref.shape
    rank, chunk = x_own_ref.shape
    part = rank // size
    rows = dy_ref.shape[0] // size
    total = dy_own_ref[...]
    for message in messages:
        total = total + message[rank:, :].astype(F32)
    for n in range(size):
        lines = total[n * part : (n + 1) * part, :]
        if rows > part:
            lines = jnp.concatenate([lines, jnp.zeros((rows - part, chunk), F32)], axis=0)
        dy_ref[n * rows : (n + 1) * rows, :] = lines
    sums = jnp.zeros((docs * rows, rank), F32)
    doc = lax.broadcasted_iota(jnp.int32, (docs, chunk), 0)
    live_tokens = jnp.zeros((docs, chunk), jnp.int32)
    for k in range(size):
        block = pos_ref[0] ^ k
        cols = pl.ds(pl.multiple_of(block * chunk, chunk), chunk)
        seg = jnp.where(doc < counts_ref[0], seg_ref[:, cols], 0)
        live_tokens = live_tokens + seg
        seg = seg.astype(F32).astype(BF16)
        dy = dy_ref[pl.ds(pl.multiple_of(block * rows, rows), rows), :]
        high = dy.astype(BF16)
        low = (dy - high.astype(F32)).astype(BF16)
        x = x_own_ref[...] if k == 0 else messages[k - 1][:rank, :]
        for piece in (high, low):
            masked = (seg[:, None, :] * piece[None, :, :]).reshape(docs * rows, chunk)
            sums = sums + lax.dot_general(masked, x, NT, preferred_element_type=F32)
    sums_ref[...] = sums
    lanes = 128 // rank
    for a in range(0, part, lanes):
        pieces = [sums_ref[pl.ds(a + n, docs, stride=rows), :] for n in range(lanes)]
        wide = pieces[0] if lanes == 1 else jnp.concatenate(pieces, axis=1)
        wide = wide.astype(BF16)
        span = slice(a * rank, (a + lanes) * rank)
        inner_ref[:, span] = wide
        shared_ref[:docs, span] = wide
    left = jnp.sum(live_tokens)
    row = lax.broadcasted_iota(jnp.int32, (DIGIT_ROWS, part * rank), 0)
    digits = jnp.zeros(row.shape, jnp.int32)
    for n, unit in enumerate(DIGITS):
        digit = left // unit
        left = left - digit * unit
        digits = jnp.where(row == n, digit, digits)
    shared_ref[docs:, :] = digits.astype(F32).astype(BF16)


def doc_sums(pos, counts, seg, dy_own, x_own, messages):
    size = len(messages) + 1
    docs, tokens = seg.shape
    rank, chunk = x_own.shape
    part = rank // size
    rows = -(-part // 16) * 16
    return pl.pallas_call(
        functools.partial(docs_kernel, size),
        in_specs=[SMEM, SMEM] + [VMEM] * (2 + size),
        out_specs=[VMEM, VMEM],
        out_shape=[
            jax.ShapeDtypeStruct((docs, part * rank), BF16),
            jax.ShapeDtypeStruct((docs + DIGIT_ROWS, part * rank), BF16),
        ],
        scratch_shapes=[
            pltpu.VMEM((rows * size, chunk), F32),
            pltpu.VMEM((docs * rows, rank), F32),
        ],
        cost_estimate=pl.CostEstimate(
            flops=4 * docs * rows * tokens * rank, bytes_accessed=1 << 20, transcendentals=0
        ),
        compiler_params=pltpu.CompilerParams(vmem_limit_bytes=16 << 20),
        name="doc_sums",
    )(pos, counts, seg, dy_own, x_own, *messages)


def fisher_kernel(shards, half_ref, *rest):
    rows, cols = rest[:shards], rest[shards : 2 * shards]
    out_ref, right_ref, tiles_ref, sems = rest[2 * shards :]
    docs, _ = rows[0].shape
    count, tile, _ = tiles_ref.shape
    total = jnp.zeros((1, 1), F32)
    for n, c in enumerate(cols):
        right_ref[n * docs : (n + 1) * docs, :] = c[:docs, :]
        digits = c[docs:, 0:1].astype(F32)
        for d, unit in enumerate(DIGITS):
            total = total + digits[d : d + 1, :] * float(unit)
    scale = 1.0 / total
    copies = []
    for t in range(count):
        lanes = pl.ds(pl.multiple_of((half_ref[0] * count + t) * tile, tile), tile)
        left = jnp.concatenate([r[:, lanes] for r in rows], axis=0)
        product = lax.dot_general(left, right_ref[...], TN, preferred_element_type=F32)
        tiles_ref[t] = product * scale
        copy = pltpu.make_async_copy(
            tiles_ref.at[t], out_ref.at[t * tile : (t + 1) * tile], sems.at[t]
        )
        copy.start()
        copies.append(copy)
    for copy in copies:
        copy.wait()


def fisher_block(half, rows, cols):
    shards = len(rows)
    docs, width = rows[0].shape
    height = width // 2
    tile = min(TILE, height)
    count = height // tile
    return pl.pallas_call(
        functools.partial(fisher_kernel, shards),
        in_specs=[SMEM] + [VMEM] * (2 * shards),
        out_specs=HBM,
        out_shape=jax.ShapeDtypeStruct((height, width), F32),
        scratch_shapes=[
            pltpu.VMEM((shards * docs, width), BF16),
            pltpu.VMEM((count, tile, width), F32),
            pltpu.SemaphoreType.DMA((count,)),
        ],
        cost_estimate=pl.CostEstimate(
            flops=2 * docs * shards * height * width,
            bytes_accessed=4 * height * width,
            transcendentals=0,
        ),
        compiler_params=pltpu.CompilerParams(vmem_limit_bytes=16 << 20),
        name="fisher_block",
    )(half, *rows, *cols)


def per_device(hidden_acts, out_grads, proj_in, proj_out, segments, doc_counts):
    size, dp_size = lax.axis_size("tensor"), lax.axis_size("dp")
    assert dp_size == 2 * size
    pos = lax.axis_index("tensor").astype(jnp.int32)
    shard = lax.axis_index("dp").astype(jnp.int32)
    pair, half = shard // 2, shard % 2
    steps = range(1, size)
    pos1, half1 = pos.reshape(1), half.reshape(1)

    proj_in_t = proj_in.T
    partials = peer_partials(pos1, hidden_acts, proj_in_t, size)
    partials = [swap(partials[k - 1], "tensor", k) for k in steps]
    x, dy_own, *dys = own_partials(
        pos1, hidden_acts, out_grads, proj_in_t, proj_out.T, size
    )
    for partial in partials:
        x = x + partial.astype(F32)
    x = x.astype(BF16)
    messages = [swap(jnp.concatenate([x, dys[k - 1]]), "tensor", k) for k in steps]
    inner, shared = doc_sums(pos1, doc_counts, segments, dy_own, x, messages)

    cols = {0: shared}
    for j in steps:
        low = j & -j
        cols[j] = swap(cols[j - low] if j != low else shared, "dp", 2 * low)
    blocks = [inner] + [swap(inner, "tensor", k) for k in steps]
    rows = []
    for j in range(size):
        where = pos ^ pair ^ j
        picked = blocks[0]
        for k in steps:
            picked = jnp.where(where == k, blocks[k], picked)
        rows.append(picked if j == 0 else swap(picked, "dp", 2 * j))
    cols = [cols[j] for j in range(size)]
    cols += [swap(c, "dp", 1) for c in cols]
    rows += [swap(r, "dp", 1) for r in rows]
    return shared[: inner.shape[0]], fisher_block(half1, rows, cols)


def solution(mesh):
    return jax.shard_map(
        per_device,
        mesh=mesh,
        in_specs=(
            P("dp", "tensor"),
            P("dp", "tensor"),
            P("tensor", None),
            P("tensor", None),
            P(None, "dp"),
            P("dp"),
        ),
        out_specs=(P("dp", "tensor"), P("dp", "tensor")),
        check_vma=False,
    )
```

```python
import functools

import jax
import jax.numpy as jnp
from jax import lax
from jax.experimental import pallas as pl
from jax.experimental.pallas import tpu as pltpu
from jax.sharding import PartitionSpec as P


BF16 = jnp.bfloat16
F32 = jnp.float32
NT = (((1,), (1,)), ((), ()))
TN = (((0,), (0,)), ((), ()))
SMEM = pl.BlockSpec(memory_space=pltpu.SMEM)
VMEM = pl.BlockSpec(memory_space=pltpu.VMEM)
HBM = pl.BlockSpec(memory_space=pltpu.HBM)
DIGITS = (65536, 256, 1)
DIGIT_LANES = 128
TILE = 128
FIRST_GRANT = 48 << 20
SECOND_GRANT = 48 << 20


def swap(value, axis, step):
    return lax.ppermute(value, axis, [(i, i ^ step) for i in range(lax.axis_size(axis))])


def stream(copies, depth, work):
    for copy in copies[:depth]:
        copy.start()
    for n, copy in enumerate(copies):
        copy.wait()
        if n + depth < len(copies):
            copies[n + depth].start()
        work(n)


def project(proj_ref, piece_ref, start, sums_ref, done):
    stop = start + piece_ref.shape[1]
    partial = lax.dot_general(
        proj_ref[:, start:stop], piece_ref[...], NT, preferred_element_type=F32
    )
    if start > 0:
        partial = sums_ref[...] + partial
    if stop < proj_ref.shape[1]:
        sums_ref[...] = partial
    else:
        done(partial)


def chunk_copies(acts_ref, block, chunk, buffers, sems, first):
    width = buffers.shape[2]
    rows = pl.ds(pl.multiple_of(block * chunk, chunk), chunk)
    return [
        pltpu.make_async_copy(
            acts_ref.at[rows, n * width : (n + 1) * width],
            buffers.at[first + n],
            sems.at[first + n],
        )
        for n in range(acts_ref.shape[1] // width)
    ]


def pieces_of(width, most):
    return max(n for n in range(1, most + 1) if width % (128 * n) == 0)


def peers_kernel(size, pos_ref, acts_ref, proj_ref, *rest):
    outs, (proj_buf, buffers, sums_ref, sems, proj_sem) = rest[: size - 1], rest[size - 1 :]
    chunk = buffers.shape[1]
    load = pltpu.make_async_copy(proj_ref, proj_buf, proj_sem)
    load.start()
    pieces = buffers.shape[0] // (size - 1)
    copies = []
    for k in range(1, size):
        block = pos_ref[0] ^ k
        copies += chunk_copies(acts_ref, block, chunk, buffers, sems, (k - 1) * pieces)

    def work(n):
        if n == 0:
            load.wait()

        def done(x):
            outs[n // pieces][...] = x.astype(BF16)

        piece = buffers.at[n]
        project(proj_buf, piece, n % pieces * piece.shape[1], sums_ref, done)

    stream(copies, 3, work)


def peer_partials(pos, acts, proj_t, size):
    tokens, width = acts.shape
    rank = proj_t.shape[0]
    chunk = tokens // size
    pieces = pieces_of(width, 2)
    count = (size - 1) * pieces
    outs = [jax.ShapeDtypeStruct((rank, chunk), BF16)] * (size - 1)
    return pl.pallas_call(
        functools.partial(peers_kernel, size),
        in_specs=[SMEM, HBM, HBM],
        out_specs=[VMEM] * len(outs),
        out_shape=outs,
        scratch_shapes=[
            pltpu.VMEM((rank, width), BF16),
            pltpu.VMEM((count, chunk, width // pieces), BF16),
            pltpu.VMEM((rank, chunk), F32),
            pltpu.SemaphoreType.DMA((count,)),
            pltpu.SemaphoreType.DMA,
        ],
        cost_estimate=pl.CostEstimate(
            flops=2 * chunk * (size - 1) * rank * width,
            bytes_accessed=2 * chunk * (size - 1) * width,
            transcendentals=0,
        ),
        compiler_params=pltpu.CompilerParams(vmem_limit_bytes=FIRST_GRANT),
        name="peer_partials",
    )(pos, acts, pltpu.with_memory_space_constraint(proj_t, pltpu.HBM))


def own_kernel(size, pos_ref, acts_ref, grads_ref, proj_in_ref, proj_out_ref, *rest):
    own_ref, dy_refs = rest[0], rest[1 : size + 1]
    weights, acts_buf, sums_ref, acts_sem = rest[size + 1 :]
    pos = pos_ref[0]
    rank = proj_out_ref.shape[0]
    part = rank // size
    chunk = acts_buf.shape[1]
    copies = chunk_copies(acts_ref, pos, chunk, acts_buf, acts_sem, 0)
    for copy in copies:
        copy.start()

    row = lax.broadcasted_iota(jnp.int32, (rank, rank), 0)
    col = lax.broadcasted_iota(jnp.int32, (rank, rank), 1)
    source = (pos ^ (row // part)) * part + row % part
    pick = jnp.where(col == source, 1.0, 0.0).astype(BF16)
    weights[...] = jnp.dot(pick, proj_out_ref[...], preferred_element_type=F32).astype(BF16)
    dy = lax.dot_general(weights[...], grads_ref[...], NT, preferred_element_type=F32)
    for m in range(size):
        for k in range(size):
            lines = dy[k * part : (k + 1) * part, m * chunk : (m + 1) * chunk]
            dy_refs[k][m * part : (m + 1) * part, :] = lines.astype(dy_refs[k].dtype)

    def done(x):
        own_ref[...] = x

    for n, copy in enumerate(copies):
        copy.wait()
        piece = acts_buf.at[n]
        project(proj_in_ref, piece, n * piece.shape[1], sums_ref, done)


def own_partials(pos, acts, grads, proj_in_t, proj_out_t, size):
    tokens, acts_width = acts.shape
    grads_width = grads.shape[1]
    rank = proj_in_t.shape[0]
    chunk = tokens // size
    pieces = pieces_of(acts_width, 2)
    return pl.pallas_call(
        functools.partial(own_kernel, size),
        in_specs=[SMEM, HBM, VMEM, VMEM, VMEM],
        out_specs=[VMEM] * (size + 1),
        out_shape=[jax.ShapeDtypeStruct((rank, chunk), F32)] * 2
        + [jax.ShapeDtypeStruct((rank, chunk), BF16)] * (size - 1),
        scratch_shapes=[
            pltpu.VMEM((rank, grads_width), BF16),
            pltpu.VMEM((pieces, chunk, acts_width // pieces), BF16),
            pltpu.VMEM((rank, chunk), F32),
            pltpu.SemaphoreType.DMA((pieces,)),
        ],
        cost_estimate=pl.CostEstimate(
            flops=2 * rank * (chunk * acts_width + tokens * grads_width),
            bytes_accessed=2 * (chunk * acts_width + tokens * grads_width),
            transcendentals=0,
        ),
        compiler_params=pltpu.CompilerParams(vmem_limit_bytes=SECOND_GRANT),
        name="own_partials",
    )(pos, acts, grads, proj_in_t, proj_out_t)


def docs_kernel(size, pos_ref, counts_ref, seg_ref, dy_own_ref, x_own_ref, *rest):
    messages = rest[: size - 1]
    inner_ref, shared_ref, dy_ref, sums_ref = rest[size - 1 :]
    docs, _ = seg_ref.shape
    rank, chunk = x_own_ref.shape
    part = rank // size
    rows = dy_ref.shape[0] // size
    total = dy_own_ref[...]
    for message in messages:
        total = total + message[rank:, :].astype(F32)
    for n in range(size):
        lines = total[n * part : (n + 1) * part, :]
        if rows > part:
            lines = jnp.concatenate([lines, jnp.zeros((rows - part, chunk), F32)], axis=0)
        dy_ref[n * rows : (n + 1) * rows, :] = lines
    sums = jnp.zeros((docs * rows, rank), F32)
    doc = lax.broadcasted_iota(jnp.int32, (docs, chunk), 0)
    live_tokens = jnp.zeros((docs, chunk), jnp.int32)
    for k in range(size):
        block = pos_ref[0] ^ k
        cols = pl.ds(pl.multiple_of(block * chunk, chunk), chunk)
        seg = jnp.where(doc < counts_ref[0], seg_ref[:, cols], 0)
        live_tokens = live_tokens + seg
        seg = seg.astype(F32).astype(BF16)
        dy = dy_ref[pl.ds(pl.multiple_of(block * rows, rows), rows), :]
        high = dy.astype(BF16)
        low = (dy - high.astype(F32)).astype(BF16)
        x = x_own_ref[...] if k == 0 else messages[k - 1][:rank, :]
        for piece in (high, low):
            masked = (seg[:, None, :] * piece[None, :, :]).reshape(docs * rows, chunk)
            sums = sums + lax.dot_general(masked, x, NT, preferred_element_type=F32)
    sums_ref[...] = sums
    lanes = 128 // rank
    for a in range(0, part, lanes):
        pieces = [sums_ref[pl.ds(a + n, docs, stride=rows), :] for n in range(lanes)]
        wide = pieces[0] if lanes == 1 else jnp.concatenate(pieces, axis=1)
        wide = wide.astype(BF16)
        span = slice(a * rank, (a + lanes) * rank)
        inner_ref[:, span] = wide
        shared_ref[:, span] = wide
    left = jnp.sum(live_tokens)
    row = lax.broadcasted_iota(jnp.int32, (docs, DIGIT_LANES), 0)
    digits = jnp.zeros(row.shape, jnp.int32)
    for n, unit in enumerate(DIGITS):
        digit = left // unit
        left = left - digit * unit
        digits = jnp.where(row == n, digit, digits)
    shared_ref[:, part * rank :] = digits.astype(F32).astype(BF16)


def doc_sums(pos, counts, seg, dy_own, x_own, messages):
    size = len(messages) + 1
    docs, tokens = seg.shape
    rank, chunk = x_own.shape
    part = rank // size
    rows = -(-part // 16) * 16
    return pl.pallas_call(
        functools.partial(docs_kernel, size),
        in_specs=[SMEM, SMEM] + [VMEM] * (2 + size),
        out_specs=[VMEM, VMEM],
        out_shape=[
            jax.ShapeDtypeStruct((docs, part * rank), BF16),
            jax.ShapeDtypeStruct((docs, part * rank + DIGIT_LANES), BF16),
        ],
        scratch_shapes=[
            pltpu.VMEM((rows * size, chunk), F32),
            pltpu.VMEM((docs * rows, rank), F32),
        ],
        cost_estimate=pl.CostEstimate(
            flops=4 * docs * rows * tokens * rank, bytes_accessed=1 << 20, transcendentals=0
        ),
        compiler_params=pltpu.CompilerParams(vmem_limit_bytes=16 << 20),
        name="doc_sums",
    )(pos, counts, seg, dy_own, x_own, *messages)


def fisher_kernel(shards, half_ref, *rest):
    rows, cols = rest[:shards], rest[shards : 2 * shards]
    out_ref, right_ref, tiles_ref, sems = rest[2 * shards :]
    docs, width = rows[0].shape
    count, tile, _ = tiles_ref.shape
    total = jnp.zeros((1, 1), F32)
    for n, c in enumerate(cols):
        right_ref[n * docs : (n + 1) * docs, :] = c[:, :width]
        digits = c[:, width : width + 1].astype(F32)
        for d, unit in enumerate(DIGITS):
            total = total + digits[d : d + 1, :] * float(unit)
    scale = 1.0 / total
    copies = []
    for t in range(count):
        lanes = pl.ds(pl.multiple_of((half_ref[0] * count + t) * tile, tile), tile)
        left = jnp.concatenate([r[:, lanes] for r in rows], axis=0)
        product = lax.dot_general(left, right_ref[...], TN, preferred_element_type=F32)
        tiles_ref[t] = product * scale
        copy = pltpu.make_async_copy(
            tiles_ref.at[t], out_ref.at[t * tile : (t + 1) * tile], sems.at[t]
        )
        copy.start()
        copies.append(copy)
    for copy in copies:
        copy.wait()


def fisher_block(half, rows, cols):
    shards = len(rows)
    docs, width = rows[0].shape
    height = width // 2
    tile = min(TILE, height)
    count = height // tile
    return pl.pallas_call(
        functools.partial(fisher_kernel, shards),
        in_specs=[SMEM] + [VMEM] * (2 * shards),
        out_specs=HBM,
        out_shape=jax.ShapeDtypeStruct((height, width), F32),
        scratch_shapes=[
            pltpu.VMEM((shards * docs, width), BF16),
            pltpu.VMEM((count, tile, width), F32),
            pltpu.SemaphoreType.DMA((count,)),
        ],
        cost_estimate=pl.CostEstimate(
            flops=2 * docs * shards * height * width,
            bytes_accessed=4 * height * width,
            transcendentals=0,
        ),
        compiler_params=pltpu.CompilerParams(vmem_limit_bytes=16 << 20),
        name="fisher_block",
    )(half, *rows, *cols)


def per_device(hidden_acts, out_grads, proj_in, proj_out, segments, doc_counts):
    size, dp_size = lax.axis_size("tensor"), lax.axis_size("dp")
    assert dp_size == 2 * size
    pos = lax.axis_index("tensor").astype(jnp.int32)
    shard = lax.axis_index("dp").astype(jnp.int32)
    pair, half = shard // 2, shard % 2
    steps = range(1, size)
    pos1, half1 = pos.reshape(1), half.reshape(1)

    proj_in_t = proj_in.T
    partials = peer_partials(pos1, hidden_acts, proj_in_t, size)
    partials = [swap(partials[k - 1], "tensor", k) for k in steps]
    x, dy_own, *dys = own_partials(
        pos1, hidden_acts, out_grads, proj_in_t, proj_out.T, size
    )
    for partial in partials:
        x = x + partial.astype(F32)
    x = x.astype(BF16)
    messages = [swap(jnp.concatenate([x, dys[k - 1]]), "tensor", k) for k in steps]
    inner, shared = doc_sums(pos1, doc_counts, segments, dy_own, x, messages)

    cols = {0: shared}
    for j in steps:
        low = j & -j
        cols[j] = swap(cols[j - low] if j != low else shared, "dp", 2 * low)
    blocks = [inner] + [swap(inner, "tensor", k) for k in steps]
    rows = []
    for j in range(size):
        where = pos ^ pair ^ j
        picked = blocks[0]
        for k in steps:
            picked = jnp.where(where == k, blocks[k], picked)
        rows.append(picked if j == 0 else swap(picked, "dp", 2 * j))
    cols = [cols[j] for j in range(size)]
    cols += [swap(c, "dp", 1) for c in cols]
    rows += [swap(r, "dp", 1) for r in rows]
    return shared[:, : inner.shape[1]], fisher_block(half1, rows, cols)


def solution(mesh):
    return jax.shard_map(
        per_device,
        mesh=mesh,
        in_specs=(
            P("dp", "tensor"),
            P("dp", "tensor"),
            P("tensor", None),
            P("tensor", None),
            P(None, "dp"),
            P("dp"),
        ),
        out_specs=(P("dp", "tensor"), P("dp", "tensor")),
        check_vma=False,
    )
```
